32 devices in a mesh: row: 8 (over y, x, core), col: 4 (over z).
Axes of the slice: x: 2, y: 2, z: 4, core: 2. Of those that a mesh axis runs over, the one named last changes fastest.
Arguments:
- teacher: bfloat16 [37, 1024, 1024], P(None, 'row', 'col'), may hold values from -320 to 320
- features: bfloat16 [64, 1024, 1024], P(None, 'row', 'col'), may hold values from -6 to 6
- valid: int32 [1024], replicated, may hold values from 0 to 1
- w_conv: bfloat16 [64, 64, 3, 3], replicated, may hold values from -0.25 to 0.25
- b_conv: float32 [64], replicated, may hold values from -3 to 3
- w_head: bfloat16 [37, 64], replicated, may hold values from -42 to 42
- b_head: float32 [37], replicated, may hold values from -4 to 4
Outputs:
- pair_loss: float32 [1024, 1024], P('row', 'col')
- loss: float32 [], replicated
- grad_conv: float32 [64, 64, 3, 3], replicated
- grad_conv_bias: float32 [64], replicated
- grad_head: float32 [37, 64], replicated
- grad_head_bias: float32 [37], replicated
The draws below stay inside these ranges and needn't reach their ends.
All inputs are finite; a program needn't handle non-finite values.
Results may differ from the reference program's by a relative error of at most 0.004.
Values may be sent and summed in bfloat16 or wider, within the bound.
A program may use at most 192 MiB of HBM per device.

```python
import jax
import jax.numpy as jnp
from jax import lax

CH = 64
BINS = 37
DILATION_STEP = 4
RESIDUE_ROWS = 128
NRES = 1024
N_ROW = 8


def draw_teacher(key, part):
    base = jnp.clip(jax.random.normal(key, (BINS, NRES, NRES), jnp.float32), -6.0, 6.0) * 3.0
    return base.astype(jnp.bfloat16)


def draw_valid(key, part):
    places = jnp.arange(NRES, dtype=jnp.int32)
    rolls = jax.random.randint(key, (NRES,), 0, 1000, dtype=jnp.int32)
    limits = 250 + 700 * places // NRES
    marks = (rolls < limits).astype(jnp.int32)
    return marks.at[0].set(1)


def draw_w_head(key, part):
    base = jnp.clip(jax.random.normal(key, (BINS, CH), jnp.float32), -4.0, 4.0) * CH ** (-0.5)
    return base.astype(jnp.bfloat16)


def block_levels(key, shape, cuts, low, high):
    gain, own = 1.0, jax.random.fold_in(key, 6)
    for position, parts in cuts:
        draws = jnp.exp(jax.random.uniform(jax.random.fold_in(own, position), (parts,), jnp.float32, low / len(cuts), high / len(cuts)))
        gain = gain * jnp.repeat(draws, shape[position] // parts).reshape([-1 if axis == position else 1 for axis in range(len(shape))])
    return gain


def normal_values(stream_key, dims, width, bound, cuts=(), held_as=jnp.bfloat16):
    array = width * jax.random.normal(stream_key, dims, jnp.float32)
    if cuts:
        array = array * block_levels(stream_key, dims, cuts, -0.22, 0.18)
    return jnp.clip(array, -bound, bound).astype(held_as)


def setup_inputs(seed: int = 0) -> dict:
    keys = jax.random.split(jax.random.key(seed), 8)
    teacher = draw_teacher(jax.random.fold_in(keys[7], 71), 0)
    features = normal_values(keys[1], (CH, NRES, NRES), 1.0, 6.0, ((1, 8), (2, 4)))
    valid = draw_valid(jax.random.fold_in(keys[7], 71), 0)
    w_conv = normal_values(keys[3], (CH, CH, 3, 3), (CH * 9) ** -0.5, 0.25)
    b_conv = normal_values(keys[4], (CH,), 0.5, 3.0, (), jnp.float32)
    w_head = draw_w_head(jax.random.fold_in(keys[7], 71), 0)
    b_head = normal_values(keys[6], (BINS,), 1.0, 4.0, (), jnp.float32)
    return {"teacher": teacher, "features": features, "valid": valid, "w_conv": w_conv, "b_conv": b_conv, "w_head": w_head, "b_head": b_head}


def reference(teacher, features, valid, w_conv, b_conv, w_head, b_head):
    total_loss = RESIDUE_ROWS * N_ROW
    padded_pairs = jnp.pad(features, ((0, 0), (DILATION_STEP, DILATION_STEP), (DILATION_STEP, DILATION_STEP)))
    valid_f = valid.astype(jnp.float32)
    kernel = w_conv.astype(jnp.float32)
    head = w_head.astype(jnp.float32)
    count = jnp.sum(valid_f) ** 2

    def band(carry, index):
        g_conv, g_cb, g_head, g_hb, l_sum = carry
        start_row = (index * RESIDUE_ROWS).astype(jnp.int32)
        pair_window = lax.dynamic_slice_in_dim(padded_pairs, start_row, RESIDUE_ROWS + 2 * DILATION_STEP, 1)
        own = lax.dynamic_slice_in_dim(teacher, start_row, RESIDUE_ROWS, 1).astype(jnp.float32)
        other = jnp.swapaxes(lax.dynamic_slice_in_dim(teacher, start_row, RESIDUE_ROWS, 2), 1, 2).astype(jnp.float32)
        target = jax.nn.softmax(0.5 * (own + other), axis=0)
        pre = lax.conv_general_dilated(pair_window[None].astype(jnp.float32), kernel, (1, 1), "VALID",
                                       rhs_dilation=(DILATION_STEP, DILATION_STEP),
                                       dimension_numbers=("NCHW", "OIHW", "NCHW"),
                                       precision=lax.Precision.HIGHEST)[0] + b_conv[:, None, None]
        act = jax.nn.elu(pre).astype(jnp.bfloat16)
        act_f = act.astype(jnp.float32)
        logits = jnp.einsum("bc,cyx->byx", head, act_f, precision=lax.Precision.HIGHEST) + b_head[:, None, None]
        logq = jax.nn.log_softmax(logits, axis=0)
        row_valid = lax.dynamic_slice_in_dim(valid_f, start_row, RESIDUE_ROWS, 0)
        weight = row_valid[:, None] * valid_f[None, :]
        cell = -weight * jnp.sum(target * logq, axis=0)
        dlog = (weight[None] * (jnp.exp(logq) - target) / total_loss).astype(jnp.bfloat16)
        dlog_f = dlog.astype(jnp.float32)
        g_hb = g_hb + jnp.sum(dlog_f, axis=(1, 2))
        g_head = g_head + jnp.einsum("byx,cyx->bc", dlog_f, act_f, precision=lax.Precision.HIGHEST)
        back = jnp.einsum("bc,byx->cyx", head, dlog_f, precision=lax.Precision.HIGHEST)
        slope = jnp.where(pre > 0, jnp.ones_like(pre), jnp.exp(jnp.minimum(pre, 0.0)))
        dpre = (back * slope).astype(jnp.bfloat16).astype(jnp.float32)
        g_cb = g_cb + jnp.sum(dpre, axis=(1, 2))
        pair_window_float = pair_window.astype(jnp.float32)
        terms = []
        for row_offset in range(3):
            for column_offset in range(3):
                shifted_pairs = pair_window_float[:, DILATION_STEP * row_offset:DILATION_STEP * row_offset + RESIDUE_ROWS, DILATION_STEP * column_offset:DILATION_STEP * column_offset + total_loss]
                terms.append(jnp.einsum("oyx,iyx->oi", dpre, shifted_pairs, precision=lax.Precision.HIGHEST))
        stacked = jnp.stack(terms).reshape(3, 3, CH, CH).transpose(2, 3, 0, 1)
        g_conv = g_conv + stacked
        l_sum = l_sum + jnp.sum(cell)
        return (g_conv, g_cb, g_head, g_hb, l_sum), cell

    init = (jnp.zeros((CH, CH, 3, 3), jnp.float32), jnp.zeros((CH,), jnp.float32),
            jnp.zeros((BINS, CH), jnp.float32), jnp.zeros((BINS,), jnp.float32), jnp.zeros((), jnp.float32))
    final, cells = lax.scan(band, init, jnp.arange(N_ROW, dtype=jnp.int32))
    g_conv, g_cb, g_head, g_hb, l_sum = final
    pair_loss = cells.reshape(total_loss, total_loss)
    return pair_loss, l_sum / count, g_conv, g_cb, g_head, g_hb
```

```python
import functools

import jax
import jax.numpy as jnp
from jax import lax
from jax.experimental import pallas as pl
from jax.experimental.pallas import tpu as pltpu
from jax.sharding import PartitionSpec as P

STEP = 4
VMEM_BYTES = 60 * 1024 * 1024


def shift_in(cells, axis, dim):
    count = lax.axis_size(axis)
    head = lax.slice_in_dim(cells, 0, STEP, axis=dim)
    tail = lax.slice_in_dim(cells, cells.shape[dim] - STEP, cells.shape[dim], axis=dim)
    before = lax.ppermute(tail, axis, [(i, i + 1) for i in range(count - 1)])
    after = lax.ppermute(head, axis, [(i + 1, i) for i in range(count - 1)])
    return before, after


def conv_kernel(rows, cols, ch, own_ref, top_ref, bottom_ref, side_ref, w_ref, b_ref, wide_ref, pre_ref):
    group = (rows + 2 * STEP) // STEP
    span = 3 * ch
    lane = lax.broadcasted_iota(jnp.int32, (ch, cols), 1)

    def widen(at, row):
        side = side_ref[at].astype(jnp.float32)
        side = jnp.concatenate([side] * (cols // 128), axis=1)
        middle = row.astype(jnp.float32)
        left = jnp.where(lane < STEP, side, pltpu.roll(middle, STEP, 1))
        right = jnp.where(lane >= cols - STEP, side, pltpu.roll(middle, cols - STEP, 1))
        start = pl.multiple_of(((at % STEP) * group + at // STEP) * span, span)
        wide_ref[pl.ds(start, ch), :] = left.astype(jnp.bfloat16)
        wide_ref[pl.ds(start + ch, ch), :] = row
        wide_ref[pl.ds(start + 2 * ch, ch), :] = right.astype(jnp.bfloat16)

    for i in range(STEP):
        widen(i, top_ref[i])
        widen(rows + STEP + i, bottom_ref[i])

    @pl.loop(0, rows, unroll=4)
    def _(y):
        widen(y + STEP, own_ref[y])

    bias = jnp.broadcast_to(b_ref[...], (ch, cols))

    @pl.loop(0, rows, unroll=4)
    def _(y):
        start = pl.multiple_of(((y % STEP) * group + y // STEP) * span, span)
        window = wide_ref[pl.ds(start, 3 * span), :]
        pre_ref[y] = jnp.dot(w_ref[...], window, preferred_element_type=jnp.float32) + bias


def rest_kernel(
    block, rows, cols, ch, bins, total,
    rv_ref, cv_ref, pre_ref, own_ref, mirror_ref, wide_ref, wh_ref, wht_ref, bh_ref,
    pair_ref, sums_ref, gw_acc, gh_acc, hb_acc, cb_acc, loss_acc,
):
    group = (rows + 2 * STEP) // STEP
    span = 3 * ch
    step = pl.program_id(0)

    @pl.when(step == 0)
    def _():
        for acc in (gw_acc, gh_acc, hb_acc, cb_acc, loss_acc):
            acc[...] = jnp.zeros_like(acc)

    bias = jnp.broadcast_to(bh_ref[...], (bins, cols))

    @pl.loop(0, block, unroll=4)
    def _(i):
        y = step * block + i
        pre = pre_ref[i]
        slope = jnp.exp(jnp.minimum(pre, 0.0))
        act = jnp.where(pre > 0, pre, slope - 1.0).astype(jnp.bfloat16)
        logits = jnp.dot(wh_ref[...], act, preferred_element_type=jnp.float32) + bias
        z = logits - jnp.max(logits, axis=0, keepdims=True)
        ez = jnp.exp(z)
        zs = jnp.sum(ez, axis=0, keepdims=True)
        logq = z - jnp.log(zs)
        sym = 0.5 * (own_ref[i].astype(jnp.float32) + mirror_ref[i].astype(jnp.float32))
        et = jnp.exp(sym - jnp.max(sym, axis=0, keepdims=True))
        target = et * (1.0 / jnp.sum(et, axis=0, keepdims=True))
        weight = rv_ref[y] * cv_ref[...]
        loss = -weight * jnp.sum(target * logq, axis=0, keepdims=True)
        pair_ref[pl.ds(i, 1), :] = loss
        loss_acc[...] += loss
        dlog = ((weight * (1.0 / total)) * (ez * (1.0 / zs) - target)).astype(jnp.bfloat16)
        hb_acc[...] += dlog.astype(jnp.float32)
        gh_acc[...] += lax.dot_general(dlog, act, (((1,), (1,)), ((), ())), preferred_element_type=jnp.float32)
        back = jnp.dot(wht_ref[...], dlog, preferred_element_type=jnp.float32)
        dpre = (back * slope).astype(jnp.bfloat16)
        cb_acc[...] += dpre.astype(jnp.float32)
        start = pl.multiple_of(((y % STEP) * group + y // STEP) * span, span)
        window = wide_ref[pl.ds(start, 3 * span), :]
        gw_acc[...] += lax.dot_general(window, dpre, (((1,), (1,)), ((), ())), preferred_element_type=jnp.float32)

    @pl.when(step == pl.num_programs(0) - 1)
    def _():
        half = 9 * ch // 2
        sums_ref[...] = jnp.zeros_like(sums_ref)
        sums_ref[0:half, 0:ch] = gw_acc[0:half, :]
        sums_ref[0:half, ch : 2 * ch] = gw_acc[half:, :]
        sums_ref[half : half + bins, 0:ch] = gh_acc[...]
        sums_ref[half : half + bins, ch : ch + 1] = jnp.sum(hb_acc[...], axis=1, keepdims=True)
        sums_ref[half + 40 : half + 40 + ch, 0:1] = jnp.sum(cb_acc[...], axis=1, keepdims=True)
        sums_ref[half + 40 : half + 41, 1:2] = jnp.sum(loss_acc[...], axis=1, keepdims=True)


def sum_kernel(n_row, n_col, chunk, x_ref, out_ref, row_slots, part, col_slots, gathered, rs_send, rs_recv, col_send, col_recv, ag_send, ag_recv):
    row, col = lax.axis_index("row"), lax.axis_index("col")
    row_peers = [lax.rem(row + o, n_row) for o in range(1, n_row)]
    col_peers = [lax.rem(col + o, n_col) for o in range(1, n_col)]
    mesh_id = pl.DeviceIdType.MESH
    barrier = pltpu.get_barrier_semaphore()
    for peer in row_peers:
        pl.semaphore_signal(barrier, inc=1, device_id=(peer, col), device_id_type=mesh_id)
    for peer in col_peers:
        pl.semaphore_signal(barrier, inc=1, device_id=(row, peer), device_id_type=mesh_id)
    pl.semaphore_wait(barrier, n_row + n_col - 2)

    def piece(index):
        return pl.ds(pl.multiple_of(index * chunk, chunk), chunk)

    def send(src, dst, send_sem, recv_sem, device):
        copy = pltpu.make_async_remote_copy(
            src_ref=src, dst_ref=dst, send_sem=send_sem, recv_sem=recv_sem, device_id=device, device_id_type=mesh_id
        )
        copy.start()
        return copy

    copies = [
        send(x_ref.at[piece(peer)], row_slots.at[o], rs_send.at[o], rs_recv.at[o], (peer, col))
        for o, peer in enumerate(row_peers)
    ]
    total = x_ref[piece(row), :]
    for o, copy in enumerate(copies):
        copy.wait_recv()
        total = total + row_slots[o]
    part[...] = total
    col_slots[col] = total
    col_copies = [
        send(part, col_slots.at[col], col_send.at[o], col_recv.at[o], (row, peer)) for o, peer in enumerate(col_peers)
    ]
    for copy in copies:
        copy.wait_send()
    for copy in col_copies:
        copy.wait_recv()
    for copy in col_copies:
        copy.wait_send()
    total = col_slots[0]
    for c in range(1, n_col):
        total = total + col_slots[c]
    part[...] = total
    gathered[piece(row), :] = total
    copies = [
        send(part, gathered.at[piece(row)], ag_send.at[o], ag_recv.at[o], (peer, col)) for o, peer in enumerate(row_peers)
    ]
    for copy in copies:
        copy.wait_recv()
    for copy in copies:
        copy.wait_send()
    out_ref[...] = gathered[...]


def summed(x):
    n_row, n_col = lax.axis_size("row"), lax.axis_size("col")
    chunk = x.shape[0] // n_row
    lanes = x.shape[1]
    dma = pltpu.SemaphoreType.DMA
    return pl.pallas_call(
        functools.partial(sum_kernel, n_row, n_col, chunk),
        name="sum_over_devices",
        out_shape=jax.ShapeDtypeStruct(x.shape, x.dtype),
        in_specs=[pl.BlockSpec(memory_space=pltpu.VMEM)],
        out_specs=pl.BlockSpec(memory_space=pltpu.VMEM),
        scratch_shapes=[
            pltpu.VMEM((n_row - 1, chunk, lanes), x.dtype),
            pltpu.VMEM((chunk, lanes), x.dtype),
            pltpu.VMEM((n_col, chunk, lanes), x.dtype),
            pltpu.VMEM(x.shape, x.dtype),
            dma((n_row - 1,)), dma((n_row - 1,)),
            dma((n_col - 1,)), dma((n_col - 1,)),
            dma((n_row - 1,)), dma((n_row - 1,)),
        ],
        compiler_params=pltpu.CompilerParams(collective_id=0, has_side_effects=True),
    )(x)

def mirrored(teacher):
    bins, rows, cols = teacher.shape
    n_row, n_col = lax.axis_size("row"), lax.axis_size("col")
    k = n_row // n_col
    ways = 4
    core = lax.axis_index("row") % k
    strip = rows // ways
    got = [[None] * ways for _ in range(k)]
    places = [(p, u, z) for p in range(n_col) for u in range(k) for z in range(n_col)]
    at = lambda p, u, z: (p * k + u) * n_col + z
    strips = []
    for d in range(ways):
        q = lax.slice_in_dim(teacher, d * strip, (d + 1) * strip, axis=1)
        if d:
            q = lax.ppermute(q, ("row", "col"), [(at(p, u, z), at(p ^ d, u, z)) for p, u, z in places])
        strips.append(q)
    for d, q in enumerate(strips):
        for e in range(k):
            half = (core + e) % k
            piece = lax.dynamic_slice_in_dim(q, half * rows, rows, 2) if k > 1 else q
            moves = [(at(p, u, z), at(z, (u + e) % k, p ^ d)) for p, u, z in places]
            got[e][d] = lax.ppermute(piece, ("row", "col"), moves)
    parts = [jnp.concatenate(g, axis=1) for g in got]
    if k == 1:
        return parts[0]
    stacked = jnp.stack(parts)
    return jnp.concatenate(
        [lax.dynamic_index_in_dim(stacked, (core - j) % k, 0, False) for j in range(k)], axis=1
    )


def on_device(teacher, features, valid, w_conv, b_conv, w_head, b_head):
    bins, rows, cols = teacher.shape
    ch = features.shape[0]
    n_row, n_col = lax.axis_size("row"), lax.axis_size("col")
    total = rows * n_row
    row_me, col_me = lax.axis_index("row"), lax.axis_index("col")

    feat = jnp.transpose(features, (1, 0, 2))
    top, bottom = shift_in(feat, "row", 0)
    edge = jnp.concatenate(
        [
            jnp.concatenate([top[:, :, :STEP], feat[:, :, :STEP], bottom[:, :, :STEP]], axis=0),
            jnp.concatenate([top[:, :, -STEP:], feat[:, :, -STEP:], bottom[:, :, -STEP:]], axis=0),
        ],
        axis=2,
    )
    left = lax.ppermute(edge[:, :, STEP:], "col", [(i, i + 1) for i in range(n_col - 1)])
    right = lax.ppermute(edge[:, :, :STEP], "col", [(i + 1, i) for i in range(n_col - 1)])
    side = jnp.concatenate([left, jnp.zeros((rows + 2 * STEP, ch, 128 - 2 * STEP), left.dtype), right], axis=2)

    mirror = mirrored(teacher)

    kernel_w = jnp.transpose(w_conv, (0, 2, 3, 1)).reshape(ch, 9 * ch)
    wide, pre = pl.pallas_call(
        functools.partial(conv_kernel, rows, cols, ch),
        name="conv_forward",
        out_shape=(
            jax.ShapeDtypeStruct(((rows + 2 * STEP) * 3 * ch, cols), jnp.bfloat16),
            jax.ShapeDtypeStruct((rows, ch, cols), jnp.float32),
        ),
        in_specs=[pl.BlockSpec(memory_space=pltpu.VMEM)] * 6,
        out_specs=(pl.BlockSpec(memory_space=pltpu.VMEM),) * 2,
        compiler_params=pltpu.CompilerParams(vmem_limit_bytes=VMEM_BYTES),
        cost_estimate=pl.CostEstimate(
            flops=2 * 9 * ch * ch * rows * cols, bytes_accessed=30_000_000, transcendentals=0
        ),
    )(feat, top, bottom, side, kernel_w, b_conv[:, None])

    mirror = jnp.transpose(mirror, (2, 0, 1))
    own = jnp.transpose(teacher, (1, 0, 2))

    valid_f = valid.astype(jnp.float32)
    count = jnp.sum(valid_f) ** 2
    row_valid = lax.dynamic_slice_in_dim(valid_f, row_me * rows, rows, 0)
    col_valid = lax.dynamic_slice_in_dim(valid_f, col_me * cols, cols, 0)

    block = 8
    half = 9 * ch // 2
    height = half + 40 + ch
    height = -(-height // (8 * n_row)) * 8 * n_row
    whole = lambda *shape: pl.BlockSpec(shape, lambda g: (0,) * len(shape), pipeline_mode=pl.Buffered(1))
    pair_loss, sums = pl.pallas_call(
        functools.partial(rest_kernel, block, rows, cols, ch, bins, total),
        name="loss_and_grads",
        grid=(rows // block,),
        out_shape=(
            jax.ShapeDtypeStruct((rows, cols), jnp.float32),
            jax.ShapeDtypeStruct((height, 2 * ch), jnp.float32),
        ),
        in_specs=[
            pl.BlockSpec(memory_space=pltpu.SMEM),
            whole(1, cols),
            pl.BlockSpec((block, ch, cols), lambda g: (g, 0, 0)),
            pl.BlockSpec((block, bins, cols), lambda g: (g, 0, 0)),
            pl.BlockSpec((block, bins, cols), lambda g: (g, 0, 0)),
            whole((rows + 2 * STEP) * 3 * ch, cols),
            whole(bins, ch),
            whole(ch, bins),
            whole(bins, 1),
        ],
        out_specs=(
            pl.BlockSpec((block, cols), lambda g: (g, 0)),
            pl.BlockSpec((height, 2 * ch), lambda g: (0, 0)),
        ),
        scratch_shapes=[
            pltpu.VMEM((9 * ch, ch), jnp.float32),
            pltpu.VMEM((bins, ch), jnp.float32),
            pltpu.VMEM((bins, cols), jnp.float32),
            pltpu.VMEM((ch, cols), jnp.float32),
            pltpu.VMEM((1, cols), jnp.float32),
        ],
        compiler_params=pltpu.CompilerParams(
            vmem_limit_bytes=VMEM_BYTES, dimension_semantics=("arbitrary",)
        ),
    )(row_valid, col_valid[None, :], pre, own, mirror, wide, w_head, w_head.T, b_head[:, None])

    sums = summed(sums)
    grad = jnp.concatenate([sums[:half, :ch], sums[:half, ch:]], axis=0)
    grad_cv = jnp.transpose(grad.reshape(3, 3, ch, ch), (3, 2, 0, 1))
    grad_hd = sums[half : half + bins, :ch]
    grad_hb = sums[half : half + bins, ch]
    grad_cb = sums[half + 40 : half + 40 + ch, 0]
    loss = sums[half + 40, 1] / count
    return (pair_loss, loss, grad_cv, grad_cb, grad_hd, grad_hb)


def solution(mesh):
    in_specs = (P(None, "row", "col"), P(None, "row", "col"), P(), P(), P(), P(), P())
    out_specs = (P("row", "col"), P(), P(), P(), P(), P())
    return jax.shard_map(
        on_device, mesh=mesh, in_specs=in_specs, out_specs=out_specs, check_vma=False
    )
```

```python
import functools

import jax
import jax.numpy as jnp
from jax import lax
from jax.experimental import pallas as pl
from jax.experimental.pallas import tpu as pltpu
from jax.sharding import PartitionSpec as P

STEP = 4
VMEM_BYTES = 60 * 1024 * 1024


def shift_in(cells, axis, dim):
    count = lax.axis_size(axis)
    head = lax.slice_in_dim(cells, 0, STEP, axis=dim)
    tail = lax.slice_in_dim(cells, cells.shape[dim] - STEP, cells.shape[dim], axis=dim)
    before = lax.ppermute(tail, axis, [(i, i + 1) for i in range(count - 1)])
    after = lax.ppermute(head, axis, [(i + 1, i) for i in range(count - 1)])
    return before, after


def conv_kernel(rows, cols, ch, own_ref, top_ref, bottom_ref, side_ref, w_ref, b_ref, wide_ref, pre_ref):
    group = (rows + 2 * STEP) // STEP
    span = 3 * ch
    lane = lax.broadcasted_iota(jnp.int32, (ch, cols), 1)

    def widen(at, row):
        side = side_ref[at].astype(jnp.float32)
        side = jnp.concatenate([side] * (cols // 128), axis=1)
        middle = row.astype(jnp.float32)
        left = jnp.where(lane < STEP, side, pltpu.roll(middle, STEP, 1))
        right = jnp.where(lane >= cols - STEP, side, pltpu.roll(middle, cols - STEP, 1))
        start = pl.multiple_of(((at % STEP) * group + at // STEP) * span, span)
        wide_ref[pl.ds(start, ch), :] = left.astype(jnp.bfloat16)
        wide_ref[pl.ds(start + ch, ch), :] = row
        wide_ref[pl.ds(start + 2 * ch, ch), :] = right.astype(jnp.bfloat16)

    for i in range(STEP):
        widen(i, top_ref[i])
        widen(rows + STEP + i, bottom_ref[i])

    @pl.loop(0, rows, unroll=4)
    def _(y):
        widen(y + STEP, own_ref[y])

    bias = jnp.broadcast_to(b_ref[...], (ch, cols))

    @pl.loop(0, rows, unroll=4)
    def _(y):
        start = pl.multiple_of(((y % STEP) * group + y // STEP) * span, span)
        window = wide_ref[pl.ds(start, 3 * span), :]
        pre_ref[y] = jnp.dot(w_ref[...], window, preferred_element_type=jnp.float32) + bias


def rest_kernel(
    wave, block, rows, cols, ch, bins, total,
    rv_ref, cv_ref, pre_ref, own_ref, mirror_ref, wide_ref, wh_ref, wht_ref, bh_ref,
    pair_ref, sums_ref, gw_acc, gh_acc, hb_acc, cb_acc, loss_acc,
):
    group = (rows + 2 * STEP) // STEP
    span = 3 * ch
    step = pl.program_id(0)

    @pl.when(step == 0)
    def _():
        for acc in (gw_acc, gh_acc, hb_acc, cb_acc, loss_acc):
            acc[...] = jnp.zeros_like(acc)

    bias = jnp.broadcast_to(bh_ref[...], (bins, wave * cols))

    def side_by_side(ref, base):
        return jnp.concatenate([ref[base + r] for r in range(wave)], axis=1)

    def folded(value):
        return functools.reduce(jnp.add, [value[:, r * cols : (r + 1) * cols] for r in range(wave)])

    def rows_at(base):
        pre = side_by_side(pre_ref, base)
        slope = jnp.exp(jnp.minimum(pre, 0.0))
        act = jnp.where(pre > 0, pre, slope - 1.0).astype(jnp.bfloat16)
        logits = jnp.dot(wh_ref[...], act, preferred_element_type=jnp.float32) + bias
        z = logits - jnp.max(logits, axis=0, keepdims=True)
        ez = jnp.exp(z)
        zs = jnp.sum(ez, axis=0, keepdims=True)
        logq = z - jnp.log(zs)
        sym = 0.5 * (
            side_by_side(own_ref, base).astype(jnp.float32) + side_by_side(mirror_ref, base).astype(jnp.float32)
        )
        et = jnp.exp(sym - jnp.max(sym, axis=0, keepdims=True))
        target = et * (1.0 / jnp.sum(et, axis=0, keepdims=True))
        y = step * block + base
        weight = jnp.concatenate([rv_ref[y + r] * cv_ref[...] for r in range(wave)], axis=1)
        loss = -weight * jnp.sum(target * logq, axis=0, keepdims=True)
        for r in range(wave):
            pair_ref[base + r : base + r + 1, :] = loss[:, r * cols : (r + 1) * cols]
        loss_acc[...] += folded(loss)
        dlog = ((weight * (1.0 / total)) * (ez * (1.0 / zs) - target)).astype(jnp.bfloat16)
        hb_acc[...] += folded(dlog.astype(jnp.float32))
        gh_acc[...] += lax.dot_general(dlog, act, (((1,), (1,)), ((), ())), preferred_element_type=jnp.float32)
        back = jnp.dot(wht_ref[...], dlog, preferred_element_type=jnp.float32)
        dpre = (back * slope).astype(jnp.bfloat16)
        cb_acc[...] += folded(dpre.astype(jnp.float32))
        windows = []
        for r in range(wave):
            place = (base + r) % STEP * group + (step * block + base + r) // STEP
            start = pl.multiple_of(place * span, span)
            windows.append(wide_ref[pl.ds(start, 3 * span), :])
        gw_acc[...] += lax.dot_general(
            jnp.concatenate(windows, axis=1), dpre, (((1,), (1,)), ((), ())), preferred_element_type=jnp.float32
        )

    for base in range(0, block, wave):
        rows_at(base)

    @pl.when(step == pl.num_programs(0) - 1)
    def _():
        half = 9 * ch // 2
        sums_ref[...] = jnp.zeros_like(sums_ref)
        sums_ref[0:half, 0:ch] = gw_acc[0:half, :]
        sums_ref[0:half, ch : 2 * ch] = gw_acc[half:, :]
        sums_ref[half : half + bins, 0:ch] = gh_acc[...]
        sums_ref[half : half + bins, ch : ch + 1] = jnp.sum(hb_acc[...], axis=1, keepdims=True)
        sums_ref[half + 40 : half + 40 + ch, 0:1] = jnp.sum(cb_acc[...], axis=1, keepdims=True)
        sums_ref[half + 40 : half + 41, 1:2] = jnp.sum(loss_acc[...], axis=1, keepdims=True)


def sum_kernel(n_row, n_col, chunk, x_ref, out_ref, row_slots, part, col_slots, gathered, rs_send, rs_recv, col_send, col_recv, ag_send, ag_recv):
    row, col = lax.axis_index("row"), lax.axis_index("col")
    row_peers = [lax.rem(row + o, n_row) for o in range(1, n_row)]
    col_peers = [lax.rem(col + o, n_col) for o in range(1, n_col)]
    mesh_id = pl.DeviceIdType.MESH
    barrier = pltpu.get_barrier_semaphore()
    for peer in row_peers:
        pl.semaphore_signal(barrier, inc=1, device_id=(peer, col), device_id_type=mesh_id)
    for peer in col_peers:
        pl.semaphore_signal(barrier, inc=1, device_id=(row, peer), device_id_type=mesh_id)
    pl.semaphore_wait(barrier, n_row + n_col - 2)

    def piece(index):
        return pl.ds(pl.multiple_of(index * chunk, chunk), chunk)

    def send(src, dst, send_sem, recv_sem, device):
        copy = pltpu.make_async_remote_copy(
            src_ref=src, dst_ref=dst, send_sem=send_sem, recv_sem=recv_sem, device_id=device, device_id_type=mesh_id
        )
        copy.start()
        return copy

    copies = [
        send(x_ref.at[piece(peer)], row_slots.at[o], rs_send.at[o], rs_recv.at[o], (peer, col))
        for o, peer in enumerate(row_peers)
    ]
    total = x_ref[piece(row), :]
    for o, copy in enumerate(copies):
        copy.wait_recv()
        total = total + row_slots[o]
    part[...] = total
    col_slots[col] = total
    col_copies = [
        send(part, col_slots.at[col], col_send.at[o], col_recv.at[o], (row, peer)) for o, peer in enumerate(col_peers)
    ]
    for copy in copies:
        copy.wait_send()
    for copy in col_copies:
        copy.wait_recv()
    for copy in col_copies:
        copy.wait_send()
    total = col_slots[0]
    for c in range(1, n_col):
        total = total + col_slots[c]
    part[...] = total
    gathered[piece(row), :] = total
    copies = [
        send(part, gathered.at[piece(row)], ag_send.at[o], ag_recv.at[o], (peer, col)) for o, peer in enumerate(row_peers)
    ]
    for copy in copies:
        copy.wait_recv()
    for copy in copies:
        copy.wait_send()
    out_ref[...] = gathered[...]


def summed(x):
    n_row, n_col = lax.axis_size("row"), lax.axis_size("col")
    chunk = x.shape[0] // n_row
    lanes = x.shape[1]
    dma = pltpu.SemaphoreType.DMA
    return pl.pallas_call(
        functools.partial(sum_kernel, n_row, n_col, chunk),
        name="sum_over_devices",
        out_shape=jax.ShapeDtypeStruct(x.shape, x.dtype),
        in_specs=[pl.BlockSpec(memory_space=pltpu.VMEM)],
        out_specs=pl.BlockSpec(memory_space=pltpu.VMEM),
        scratch_shapes=[
            pltpu.VMEM((n_row - 1, chunk, lanes), x.dtype),
            pltpu.VMEM((chunk, lanes), x.dtype),
            pltpu.VMEM((n_col, chunk, lanes), x.dtype),
            pltpu.VMEM(x.shape, x.dtype),
            dma((n_row - 1,)), dma((n_row - 1,)),
            dma((n_col - 1,)), dma((n_col - 1,)),
            dma((n_row - 1,)), dma((n_row - 1,)),
        ],
        compiler_params=pltpu.CompilerParams(collective_id=0, has_side_effects=True),
    )(x)

def mirrored(teacher):
    bins, rows, cols = teacher.shape
    n_row, n_col = lax.axis_size("row"), lax.axis_size("col")
    k = n_row // n_col
    ways = 4
    core = lax.axis_index("row") % k
    strip = rows // ways
    got = [[None] * ways for _ in range(k)]
    places = [(p, u, z) for p in range(n_col) for u in range(k) for z in range(n_col)]
    at = lambda p, u, z: (p * k + u) * n_col + z
    strips = []
    for d in range(ways):
        q = lax.slice_in_dim(teacher, d * strip, (d + 1) * strip, axis=1)
        if d:
            q = lax.ppermute(q, ("row", "col"), [(at(p, u, z), at(p ^ d, u, z)) for p, u, z in places])
        strips.append(q)
    for d, q in enumerate(strips):
        for e in range(k):
            half = (core + e) % k
            piece = lax.dynamic_slice_in_dim(q, half * rows, rows, 2) if k > 1 else q
            moves = [(at(p, u, z), at(z, (u + e) % k, p ^ d)) for p, u, z in places]
            got[e][d] = lax.ppermute(piece, ("row", "col"), moves)
    parts = [jnp.concatenate(g, axis=1) for g in got]
    if k == 1:
        return parts[0]
    stacked = jnp.stack(parts)
    return jnp.concatenate(
        [lax.dynamic_index_in_dim(stacked, (core - j) % k, 0, False) for j in range(k)], axis=1
    )


def on_device(teacher, features, valid, w_conv, b_conv, w_head, b_head):
    bins, rows, cols = teacher.shape
    ch = features.shape[0]
    n_row, n_col = lax.axis_size("row"), lax.axis_size("col")
    total = rows * n_row
    row_me, col_me = lax.axis_index("row"), lax.axis_index("col")

    feat = jnp.transpose(features, (1, 0, 2))
    top, bottom = shift_in(feat, "row", 0)
    edge = jnp.concatenate(
        [
            jnp.concatenate([top[:, :, :STEP], feat[:, :, :STEP], bottom[:, :, :STEP]], axis=0),
            jnp.concatenate([top[:, :, -STEP:], feat[:, :, -STEP:], bottom[:, :, -STEP:]], axis=0),
        ],
        axis=2,
    )
    left = lax.ppermute(edge[:, :, STEP:], "col", [(i, i + 1) for i in range(n_col - 1)])
    right = lax.ppermute(edge[:, :, :STEP], "col", [(i + 1, i) for i in range(n_col - 1)])
    side = jnp.concatenate([left, jnp.zeros((rows + 2 * STEP, ch, 128 - 2 * STEP), left.dtype), right], axis=2)

    mirror = mirrored(teacher)

    kernel_w = jnp.transpose(w_conv, (0, 2, 3, 1)).reshape(ch, 9 * ch)
    wide, pre = pl.pallas_call(
        functools.partial(conv_kernel, rows, cols, ch),
        name="conv_forward",
        out_shape=(
            jax.ShapeDtypeStruct(((rows + 2 * STEP) * 3 * ch, cols), jnp.bfloat16),
            jax.ShapeDtypeStruct((rows, ch, cols), jnp.float32),
        ),
        in_specs=[pl.BlockSpec(memory_space=pltpu.VMEM)] * 6,
        out_specs=(pl.BlockSpec(memory_space=pltpu.VMEM),) * 2,
        compiler_params=pltpu.CompilerParams(vmem_limit_bytes=VMEM_BYTES),
        cost_estimate=pl.CostEstimate(
            flops=2 * 9 * ch * ch * rows * cols, bytes_accessed=30_000_000, transcendentals=0
        ),
    )(feat, top, bottom, side, kernel_w, b_conv[:, None])

    mirror = jnp.transpose(mirror, (2, 0, 1))
    own = jnp.transpose(teacher, (1, 0, 2))

    valid_f = valid.astype(jnp.float32)
    count = jnp.sum(valid_f) ** 2
    row_valid = lax.dynamic_slice_in_dim(valid_f, row_me * rows, rows, 0)
    col_valid = lax.dynamic_slice_in_dim(valid_f, col_me * cols, cols, 0)

    block, wave = 16, 4
    half = 9 * ch // 2
    height = half + 40 + ch
    height = -(-height // (8 * n_row)) * 8 * n_row
    whole = lambda *shape: pl.BlockSpec(shape, lambda g: (0,) * len(shape), pipeline_mode=pl.Buffered(1))
    pair_loss, sums = pl.pallas_call(
        functools.partial(rest_kernel, wave, block, rows, cols, ch, bins, total),
        name="loss_and_grads",
        grid=(rows // block,),
        out_shape=(
            jax.ShapeDtypeStruct((rows, cols), jnp.float32),
            jax.ShapeDtypeStruct((height, 2 * ch), jnp.float32),
        ),
        in_specs=[
            pl.BlockSpec(memory_space=pltpu.SMEM),
            whole(1, cols),
            pl.BlockSpec((block, ch, cols), lambda g: (g, 0, 0)),
            pl.BlockSpec((block, bins, cols), lambda g: (g, 0, 0)),
            pl.BlockSpec((block, bins, cols), lambda g: (g, 0, 0)),
            whole((rows + 2 * STEP) * 3 * ch, cols),
            whole(bins, ch),
            whole(ch, bins),
            whole(bins, 1),
        ],
        out_specs=(
            pl.BlockSpec((block, cols), lambda g: (g, 0)),
            pl.BlockSpec((height, 2 * ch), lambda g: (0, 0)),
        ),
        scratch_shapes=[
            pltpu.VMEM((9 * ch, ch), jnp.float32),
            pltpu.VMEM((bins, ch), jnp.float32),
            pltpu.VMEM((bins, cols), jnp.float32),
            pltpu.VMEM((ch, cols), jnp.float32),
            pltpu.VMEM((1, cols), jnp.float32),
        ],
        compiler_params=pltpu.CompilerParams(
            vmem_limit_bytes=VMEM_BYTES, dimension_semantics=("arbitrary",)
        ),
    )(row_valid, col_valid[None, :], pre, own, mirror, wide, w_head, w_head.T, b_head[:, None])

    sums = summed(sums)
    grad = jnp.concatenate([sums[:half, :ch], sums[:half, ch:]], axis=0)
    grad_cv = jnp.transpose(grad.reshape(3, 3, ch, ch), (3, 2, 0, 1))
    grad_hd = sums[half : half + bins, :ch]
    grad_hb = sums[half : half + bins, ch]
    grad_cb = sums[half + 40 : half + 40 + ch, 0]
    loss = sums[half + 40, 1] / count
    return (pair_loss, loss, grad_cv, grad_cb, grad_hd, grad_hb)


def solution(mesh):
    in_specs = (P(None, "row", "col"), P(None, "row", "col"), P(), P(), P(), P(), P())
    out_specs = (P("row", "col"), P(), P(), P(), P(), P())
    return jax.shard_map(
        on_device, mesh=mesh, in_specs=in_specs, out_specs=out_specs, check_vma=False
    )
```

```python
import functools

import jax
import jax.numpy as jnp
from jax import lax
from jax.experimental import pallas as pl
from jax.experimental.pallas import tpu as pltpu
from jax.sharding import PartitionSpec as P

STEP = 4
VMEM_BYTES = 60 * 1024 * 1024


def shift_in(cells, axis, dim):
    count = lax.axis_size(axis)
    head = lax.slice_in_dim(cells, 0, STEP, axis=dim)
    tail = lax.slice_in_dim(cells, cells.shape[dim] - STEP, cells.shape[dim], axis=dim)
    before = lax.ppermute(tail, axis, [(i, i + 1) for i in range(count - 1)])
    after = lax.ppermute(head, axis, [(i + 1, i) for i in range(count - 1)])
    return before, after


def conv_kernel(rows, cols, ch, own_ref, top_ref, bottom_ref, side_ref, w_ref, b_ref, wide_ref, pre_ref):
    group = (rows + 2 * STEP) // STEP
    span = 3 * ch
    lane = lax.broadcasted_iota(jnp.int32, (ch, cols), 1)

    def widen(at, row):
        side = side_ref[at].astype(jnp.float32)
        side = jnp.concatenate([side] * (cols // 128), axis=1)
        middle = row.astype(jnp.float32)
        left = jnp.where(lane < STEP, side, pltpu.roll(middle, STEP, 1))
        right = jnp.where(lane >= cols - STEP, side, pltpu.roll(middle, cols - STEP, 1))
        start = pl.multiple_of(((at % STEP) * group + at // STEP) * span, span)
        wide_ref[pl.ds(start, ch), :] = left.astype(jnp.bfloat16)
        wide_ref[pl.ds(start + ch, ch), :] = row
        wide_ref[pl.ds(start + 2 * ch, ch), :] = right.astype(jnp.bfloat16)

    for i in range(STEP):
        widen(i, top_ref[i])
        widen(rows + STEP + i, bottom_ref[i])

    @pl.loop(0, rows, unroll=4)
    def _(y):
        widen(y + STEP, own_ref[y])

    bias = jnp.broadcast_to(b_ref[...], (ch, cols))

    @pl.loop(0, rows, unroll=4)
    def _(y):
        start = pl.multiple_of(((y % STEP) * group + y // STEP) * span, span)
        window = wide_ref[pl.ds(start, 3 * span), :]
        pre_ref[y] = jnp.dot(w_ref[...], window, preferred_element_type=jnp.float32) + bias


def rest_kernel(
    wave, block, rows, cols, ch, bins, total,
    rv_ref, cv_ref, pre_ref, own_ref, mirror_ref, wide_ref, wh_ref, wht_ref, bh_ref,
    pair_ref, sums_ref, gw_acc, gh_acc, hb_acc, cb_acc, loss_acc,
):
    group = (rows + 2 * STEP) // STEP
    span = 3 * ch
    step = pl.program_id(0)

    @pl.when(step == 0)
    def _():
        for acc in (gw_acc, gh_acc, hb_acc, cb_acc, loss_acc):
            acc[...] = jnp.zeros_like(acc)

    bias = jnp.broadcast_to(bh_ref[...], (bins, wave * cols))

    def side_by_side(ref, base):
        return jnp.concatenate([ref[base + r] for r in range(wave)], axis=1)

    def folded(value):
        return functools.reduce(jnp.add, [value[:, r * cols : (r + 1) * cols] for r in range(wave)])

    def rows_at(base):
        pre = side_by_side(pre_ref, base)
        slope = jnp.exp(jnp.minimum(pre, 0.0))
        act = jnp.where(pre > 0, pre, slope - 1.0).astype(jnp.bfloat16)
        logits = jnp.dot(wh_ref[...], act, preferred_element_type=jnp.float32) + bias
        z = logits - jnp.max(logits, axis=0, keepdims=True)
        ez = jnp.exp(z)
        zs = jnp.sum(ez, axis=0, keepdims=True)
        logq = z - jnp.log(zs)
        sym = 0.5 * (
            side_by_side(own_ref, base).astype(jnp.float32) + side_by_side(mirror_ref, base).astype(jnp.float32)
        )
        et = jnp.exp(sym - jnp.max(sym, axis=0, keepdims=True))
        target = et * (1.0 / jnp.sum(et, axis=0, keepdims=True))
        y = step * block + base
        weight = jnp.concatenate([rv_ref[y + r] * cv_ref[...] for r in range(wave)], axis=1)
        loss = -weight * jnp.sum(target * logq, axis=0, keepdims=True)
        for r in range(wave):
            pair_ref[base + r : base + r + 1, :] = loss[:, r * cols : (r + 1) * cols]
        loss_acc[...] += folded(loss)
        dlog = ((weight * (1.0 / total)) * (ez * (1.0 / zs) - target)).astype(jnp.bfloat16)
        hb_acc[...] += folded(dlog.astype(jnp.float32))
        gh_acc[...] += lax.dot_general(dlog, act, (((1,), (1,)), ((), ())), preferred_element_type=jnp.float32)
        back = jnp.dot(wht_ref[...], dlog, preferred_element_type=jnp.float32)
        dpre = (back * slope).astype(jnp.bfloat16)
        cb_acc[...] += folded(dpre.astype(jnp.float32))
        windows = []
        for r in range(wave):
            place = (base + r) % STEP * group + (step * block + base + r) // STEP
            start = pl.multiple_of(place * span, span)
            windows.append(wide_ref[pl.ds(start, 3 * span), :])
        gw_acc[...] += lax.dot_general(
            jnp.concatenate(windows, axis=1), dpre, (((1,), (1,)), ((), ())), preferred_element_type=jnp.float32
        )

    for base in range(0, block, wave):
        rows_at(base)

    @pl.when(step == pl.num_programs(0) - 1)
    def _():
        half = 9 * ch // 2
        sums_ref[...] = jnp.zeros_like(sums_ref)
        sums_ref[0:half, 0:ch] = gw_acc[0:half, :]
        sums_ref[0:half, ch : 2 * ch] = gw_acc[half:, :]
        sums_ref[half : half + bins, 0:ch] = gh_acc[...]
        sums_ref[half : half + bins, ch : ch + 1] = jnp.sum(hb_acc[...], axis=1, keepdims=True)
        sums_ref[half + 40 : half + 40 + ch, 0:1] = jnp.sum(cb_acc[...], axis=1, keepdims=True)
        sums_ref[half + 40 : half + 41, 1:2] = jnp.sum(loss_acc[...], axis=1, keepdims=True)


def sum_kernel(n_row, n_col, chunk, x_ref, out_ref, row_slots, part, col_slots, gathered, rs_send, rs_recv, col_send, col_recv, ag_send, ag_recv):
    row, col = lax.axis_index("row"), lax.axis_index("col")
    row_peers = [lax.rem(row + o, n_row) for o in range(1, n_row)]
    col_peers = [lax.rem(col + o, n_col) for o in range(1, n_col)]
    mesh_id = pl.DeviceIdType.MESH
    barrier = pltpu.get_barrier_semaphore()
    for peer in row_peers:
        pl.semaphore_signal(barrier, inc=1, device_id=(peer, col), device_id_type=mesh_id)
    for peer in col_peers:
        pl.semaphore_signal(barrier, inc=1, device_id=(row, peer), device_id_type=mesh_id)
    pl.semaphore_wait(barrier, n_row + n_col - 2)

    def piece(index):
        return pl.ds(pl.multiple_of(index * chunk, chunk), chunk)

    def send(src, dst, send_sem, recv_sem, device):
        copy = pltpu.make_async_remote_copy(
            src_ref=src, dst_ref=dst, send_sem=send_sem, recv_sem=recv_sem, device_id=device, device_id_type=mesh_id
        )
        copy.start()
        return copy

    copies = [
        send(x_ref.at[piece(peer)], row_slots.at[o], rs_send.at[o], rs_recv.at[o], (peer, col))
        for o, peer in enumerate(row_peers)
    ]
    total = x_ref[piece(row), :]
    for o, copy in enumerate(copies):
        copy.wait_recv()
        total = total + row_slots[o]
    part[...] = total
    col_slots[col] = total
    col_copies = [
        send(part, col_slots.at[col], col_send.at[o], col_recv.at[o], (row, peer)) for o, peer in enumerate(col_peers)
    ]
    for copy in copies:
        copy.wait_send()
    for copy in col_copies:
        copy.wait_recv()
    for copy in col_copies:
        copy.wait_send()
    total = col_slots[0]
    for c in range(1, n_col):
        total = total + col_slots[c]
    part[...] = total
    gathered[piece(row), :] = total
    copies = [
        send(part, gathered.at[piece(row)], ag_send.at[o], ag_recv.at[o], (peer, col)) for o, peer in enumerate(row_peers)
    ]
    for copy in copies:
        copy.wait_recv()
    for copy in copies:
        copy.wait_send()
    out_ref[...] = gathered[...]


def summed(x):
    n_row, n_col = lax.axis_size("row"), lax.axis_size("col")
    chunk = x.shape[0] // n_row
    lanes = x.shape[1]
    dma = pltpu.SemaphoreType.DMA
    return pl.pallas_call(
        functools.partial(sum_kernel, n_row, n_col, chunk),
        name="sum_over_devices",
        out_shape=jax.ShapeDtypeStruct(x.shape, x.dtype),
        in_specs=[pl.BlockSpec(memory_space=pltpu.VMEM)],
        out_specs=pl.BlockSpec(memory_space=pltpu.VMEM),
        scratch_shapes=[
            pltpu.VMEM((n_row - 1, chunk, lanes), x.dtype),
            pltpu.VMEM((chunk, lanes), x.dtype),
            pltpu.VMEM((n_col, chunk, lanes), x.dtype),
            pltpu.VMEM(x.shape, x.dtype),
            dma((n_row - 1,)), dma((n_row - 1,)),
            dma((n_col - 1,)), dma((n_col - 1,)),
            dma((n_row - 1,)), dma((n_row - 1,)),
        ],
        compiler_params=pltpu.CompilerParams(collective_id=0, has_side_effects=True),
    )(x)

def mirrored(teacher, pre):
    bins, rows, cols = teacher.shape
    n_row, n_col = lax.axis_size("row"), lax.axis_size("col")
    k = n_row // n_col
    ways = 4
    core = lax.axis_index("row") % k
    strip = rows // ways
    got = [[None] * ways for _ in range(k)]
    places = [(p, u, z) for p in range(n_col) for u in range(k) for z in range(n_col)]
    at = lambda p, u, z: (p * k + u) * n_col + z
    strips = []
    for d in range(ways):
        q = lax.slice_in_dim(teacher, d * strip, (d + 1) * strip, axis=1)
        if d:
            q = lax.ppermute(q, ("row", "col"), [(at(p, u, z), at(p ^ d, u, z)) for p, u, z in places])
        strips.append(q)
    strips[2], strips[3], pre = lax.optimization_barrier((strips[2], strips[3], pre))
    for d, q in enumerate(strips):
        for e in range(k):
            half = (core + e) % k
            piece = lax.dynamic_slice_in_dim(q, half * rows, rows, 2) if k > 1 else q
            moves = [(at(p, u, z), at(z, (u + e) % k, p ^ d)) for p, u, z in places]
            got[e][d] = lax.ppermute(piece, ("row", "col"), moves)
    parts = [jnp.concatenate(g, axis=1) for g in got]
    if k == 1:
        return parts[0], pre
    stacked = jnp.stack(parts)
    ordered = [lax.dynamic_index_in_dim(stacked, (core - j) % k, 0, False) for j in range(k)]
    return jnp.concatenate(ordered, axis=1), pre


def on_device(teacher, features, valid, w_conv, b_conv, w_head, b_head):
    bins, rows, cols = teacher.shape
    ch = features.shape[0]
    n_row, n_col = lax.axis_size("row"), lax.axis_size("col")
    total = rows * n_row
    row_me, col_me = lax.axis_index("row"), lax.axis_index("col")

    feat = jnp.transpose(features, (1, 0, 2))
    top, bottom = shift_in(feat, "row", 0)
    edge = jnp.concatenate(
        [
            jnp.concatenate([top[:, :, :STEP], feat[:, :, :STEP], bottom[:, :, :STEP]], axis=0),
            jnp.concatenate([top[:, :, -STEP:], feat[:, :, -STEP:], bottom[:, :, -STEP:]], axis=0),
        ],
        axis=2,
    )
    left = lax.ppermute(edge[:, :, STEP:], "col", [(i, i + 1) for i in range(n_col - 1)])
    right = lax.ppermute(edge[:, :, :STEP], "col", [(i + 1, i) for i in range(n_col - 1)])
    side = jnp.concatenate([left, jnp.zeros((rows + 2 * STEP, ch, 128 - 2 * STEP), left.dtype), right], axis=2)


    kernel_w = jnp.transpose(w_conv, (0, 2, 3, 1)).reshape(ch, 9 * ch)
    wide, pre = pl.pallas_call(
        functools.partial(conv_kernel, rows, cols, ch),
        name="conv_forward",
        out_shape=(
            jax.ShapeDtypeStruct(((rows + 2 * STEP) * 3 * ch, cols), jnp.bfloat16),
            jax.ShapeDtypeStruct((rows, ch, cols), jnp.float32),
        ),
        in_specs=[pl.BlockSpec(memory_space=pltpu.VMEM)] * 6,
        out_specs=(pl.BlockSpec(memory_space=pltpu.VMEM),) * 2,
        compiler_params=pltpu.CompilerParams(vmem_limit_bytes=VMEM_BYTES),
        cost_estimate=pl.CostEstimate(
            flops=2 * 9 * ch * ch * rows * cols, bytes_accessed=30_000_000, transcendentals=0
        ),
    )(feat, top, bottom, side, kernel_w, b_conv[:, None])

    mirror, pre = mirrored(teacher, pre)
    mirror = jnp.transpose(mirror, (2, 0, 1))
    own = jnp.transpose(teacher, (1, 0, 2))

    valid_f = valid.astype(jnp.float32)
    count = jnp.sum(valid_f) ** 2
    row_valid = lax.dynamic_slice_in_dim(valid_f, row_me * rows, rows, 0)
    col_valid = lax.dynamic_slice_in_dim(valid_f, col_me * cols, cols, 0)

    block, wave = 16, 4
    half = 9 * ch // 2
    height = half + 40 + ch
    height = -(-height // (8 * n_row)) * 8 * n_row
    whole = lambda *shape: pl.BlockSpec(shape, lambda g: (0,) * len(shape), pipeline_mode=pl.Buffered(1))
    pair_loss, sums = pl.pallas_call(
        functools.partial(rest_kernel, wave, block, rows, cols, ch, bins, total),
        name="loss_and_grads",
        grid=(rows // block,),
        out_shape=(
            jax.ShapeDtypeStruct((rows, cols), jnp.float32),
            jax.ShapeDtypeStruct((height, 2 * ch), jnp.float32),
        ),
        in_specs=[
            pl.BlockSpec(memory_space=pltpu.SMEM),
            whole(1, cols),
            pl.BlockSpec((block, ch, cols), lambda g: (g, 0, 0)),
            pl.BlockSpec((block, bins, cols), lambda g: (g, 0, 0)),
            pl.BlockSpec((block, bins, cols), lambda g: (g, 0, 0)),
            whole((rows + 2 * STEP) * 3 * ch, cols),
            whole(bins, ch),
            whole(ch, bins),
            whole(bins, 1),
        ],
        out_specs=(
            pl.BlockSpec((block, cols), lambda g: (g, 0)),
            pl.BlockSpec((height, 2 * ch), lambda g: (0, 0)),
        ),
        scratch_shapes=[
            pltpu.VMEM((9 * ch, ch), jnp.float32),
            pltpu.VMEM((bins, ch), jnp.float32),
            pltpu.VMEM((bins, cols), jnp.float32),
            pltpu.VMEM((ch, cols), jnp.float32),
            pltpu.VMEM((1, cols), jnp.float32),
        ],
        compiler_params=pltpu.CompilerParams(
            vmem_limit_bytes=VMEM_BYTES, dimension_semantics=("arbitrary",)
        ),
    )(row_valid, col_valid[None, :], pre, own, mirror, wide, w_head, w_head.T, b_head[:, None])

    sums = summed(sums)
    grad = jnp.concatenate([sums[:half, :ch], sums[:half, ch:]], axis=0)
    grad_cv = jnp.transpose(grad.reshape(3, 3, ch, ch), (3, 2, 0, 1))
    grad_hd = sums[half : half + bins, :ch]
    grad_hb = sums[half : half + bins, ch]
    grad_cb = sums[half + 40 : half + 40 + ch, 0]
    loss = sums[half + 40, 1] / count
    return (pair_loss, loss, grad_cv, grad_cb, grad_hd, grad_hb)


def solution(mesh):
    in_specs = (P(None, "row", "col"), P(None, "row", "col"), P(), P(), P(), P(), P())
    out_specs = (P("row", "col"), P(), P(), P(), P(), P())
    return jax.shard_map(
        on_device, mesh=mesh, in_specs=in_specs, out_specs=out_specs, check_vma=False
    )
```
